256 devices in a mesh: lang: 4 (over x_hi, core), blk: 64 (over x_lo, z, y).
Axes of the slice: x: 4 (x_hi: 2, x_lo: 2; x = x_hi * 2 + x_lo), y: 4, z: 8, core: 2. Of those that a mesh axis runs over, the one named last changes fastest.
Arguments:
- fisher: bfloat16 [8, 4096, 16384], P('lang', None, 'blk'), may hold values from 0.049804688 to 5
- factor_left: bfloat16 [8, 4096, 64], P('lang', 'blk'), may hold values from -6 to 6
- factor_right: bfloat16 [8, 64, 16384], P('lang', None, 'blk'), may hold values from -0.75 to 0.75
- base_weight: bfloat16 [4096, 16384], P(('lang', 'blk')), may hold values from -3 to 3
Outputs:
- merged: bfloat16 [4096, 16384], P(('lang', 'blk'))
The draws below stay inside these ranges and needn't reach their ends.
All inputs are finite; a program needn't handle non-finite values.
Results may differ from the reference program's by a relative error of at most 0.0011.
Values may be sent and summed in bfloat16 or wider, within the bound.
A program may use at most 128 MiB of HBM per device.

```python
import math
import jax
import jax.numpy as jnp
from jax import lax

D = 4096
FFW = 16384
R = 64
LANGS = 8


def shard_levels(key, extent, split, low, top_value):
    def one(position, parts):
        steps = jax.random.uniform(jax.random.fold_in(jax.random.fold_in(key, 6), position), (parts,), jnp.float32, low / len(split), top_value / len(split))
        return jnp.repeat(jnp.exp(steps), extent[position] // parts).reshape((-1,) + (1,) * (len(extent) - position - 1))

    level = one(*split[0])
    for cut in split[1:]:
        level = level * one(*cut)
    return level


def noise(key, shape, scale, limit, split=(), kind=jnp.bfloat16):
    factor_of = shard_levels(key, shape, split, -0.22, 0.18) if split else 1.0
    values = jax.random.normal(key, shape, jnp.float32) * scale * factor_of
    return jnp.minimum(jnp.maximum(values, -limit), limit).astype(kind)


def setup_inputs(seed: int = 0) -> dict:
    key_list = jax.random.split(jax.random.key(seed), 5)
    return {
        "fisher": jnp.clip(jnp.exp(math.log(5.0) - 4.609084 * jax.random.uniform(key_list[0], (LANGS, D, FFW), jnp.float32) ** shard_levels(key_list[0], (LANGS, D, FFW), ((0, 4), (2, 64)), -0.2, 0.2)), 0.049804688, 5.0).astype(jnp.bfloat16),
        "factor_left": noise(key_list[1], (LANGS, D, R), 1.0, 6.0, ((0, 4), (1, 64))),
        "factor_right": noise(key_list[2], (LANGS, R, FFW), R ** -0.5, 0.75, ((0, 4), (2, 64))),
        "base_weight": noise(key_list[3], (D, FFW), 0.5, 3.0, ((0, 256),)),
    }


def reference(fisher, factor_left, factor_right, base_weight):
    def add_language(carry, inputs):
        weighted, totals = carry
        weight, left, right = inputs
        change = jnp.dot(left, right, preferred_element_type=jnp.float32)
        weight_wide = weight.astype(jnp.float32)
        return (weighted + weight_wide * change, totals + weight_wide), None

    zeros = jnp.zeros(base_weight.shape, jnp.float32)
    (weighted, totals), _ = lax.scan(add_language, (zeros, zeros), (fisher, factor_left, factor_right))
    return (base_weight.astype(jnp.float32) + weighted / totals).astype(jnp.bfloat16)
```

```python
import jax
import jax.numpy as jnp
from jax import lax
from jax.experimental import pallas as pl
from jax.experimental.pallas import tpu as pltpu
from jax.sharding import PartitionSpec as P

BF16, F32 = jnp.bfloat16, jnp.float32
NZ, NY = 8, 4
LAG = 3
W_KNEE, W_SCALE = 0.25, 2.0**-7.25
D_KNEE, D_SCALE = 0.01, 2.0**-7.4


def encode(v, knee, scale):
    c = jnp.abs(v) * (scale / knee) + scale
    c = c * c
    c = c * c
    c = c * c
    c = c * c
    return jnp.where(v < 0, -c, c).astype(BF16)


def root16(y):
    return jnp.exp2(jnp.log2(y) * (1.0 / 16))


def decode(y, knee, scale):
    y = y.astype(F32)
    v = root16(jnp.abs(y)) * (knee / scale) - knee
    return jnp.where(y < 0, -v, v)


def encode_total(t):
    c = t * 0.5
    c = c * c
    c = c * c
    c = c * c
    return (c * c).astype(BF16)


def decode_total(y):
    return root16(y.astype(F32)) * 2.0


def kernel(fisher, left, right, base, out, packed, lefts, rights, weights, fish, sent, own, got, delta_out, delta_in,
           f_local, f_send, f_recv, r_sem, l_send, l_first, l_recv, y_send, y_recv, x_send, x_recv, d_send, d_recv):
    lang, blk = lax.axis_index("lang"), lax.axis_index("blk")
    xh, core = lang // 2, lang % 2
    xl, z, y = blk // 32, (blk // 4) % 8, blk % 4
    x = 2 * xh + xl
    zc = z // 4
    other = 1 - core

    def dev(xh_, c_, xl_, z_, y_):
        return {"lang": 2 * xh_ + c_, "blk": 32 * xl_ + 4 * z_ + y_}

    def remote(src, dst, send, recv, device):
        return pltpu.make_async_remote_copy(
            src_ref=src, dst_ref=dst, send_sem=send, recv_sem=recv, device_id=device, device_id_type=pl.DeviceIdType.MESH
        )

    barrier = pltpu.get_barrier_semaphore()

    def greet(device):
        pl.semaphore_signal(barrier, inc=1, device_id=device, device_id_type=pl.DeviceIdType.MESH)

    greet(dev(1 - xh, core, xl, z, y))
    greet(dev(1 - xh, core, 1 - xl, z, y))
    greet(dev(xh, other, xl, z, y))

    def greet_line(k, carry):
        greet(dev(xh, (core + k // 16) % 2, (xl + (k // 8) % 2) % 2, (z + k) % 8, y))
        return carry

    lax.fori_loop(1, 16, greet_line, 0)
    lax.fori_loop(17, 32, greet_line, 0)

    def greet_plane(k, carry):
        greet(dev(xh, core, xl, (z + k) % 8, (y + 1 + k // 8) % 4))
        return carry

    lax.fori_loop(0, 24, greet_plane, 0)

    def rows(g, c_):
        return pl.ds(pl.multiple_of(1024 * (2 * (g // 2) + c_) + 512 * (g % 2), 512), 512)

    local = [pltpu.make_async_copy(fisher.at[:, rows(g, core), :], fish.at[g, core], f_local.at[g]) for g in range(4)]
    for copy in local:
        copy.start()
    r_local = pltpu.make_async_copy(right, rights.at[core], r_sem.at[0])
    r_local.start()
    packed[...] = jnp.concatenate([left[0], left[1]], axis=1)
    weights[...] = jnp.zeros_like(weights)
    pl.semaphore_wait(barrier, 57)

    g_own = 2 * xl + (z // 2) % 2
    zb_own = z % 2
    slot = lefts.at[g_own, zb_own * 4 + y, core]
    slot_sem = l_recv.at[g_own * 2 + zb_own, core]
    first_local = pltpu.make_async_copy(packed, slot, slot_sem)
    first_remote = remote(packed, slot, l_first, slot_sem, dev(xh, zc, xl, z, y))

    @pl.when(zc == core)
    def _():
        first_local.start()

    @pl.when(zc != core)
    def _():
        first_remote.start()

    def left_copy(k):
        return remote(packed, slot, l_send.at[k], slot_sem, dev(xh, zc, (xl + k // 8) % 2, (z + k) % 8, y))

    def left_start(k, carry):
        left_copy(k).start()
        return carry

    lax.fori_loop(1, 16, left_start, 0)

    r_remote = remote(right, rights.at[core], r_sem.at[1], r_sem.at[2], dev(xh, other, xl, z, y))
    r_remote.start()
    f_remote = [
        remote(fisher.at[:, rows(g, other), :], fish.at[g, core], f_send.at[g], f_recv.at[g], dev(xh, other, xl, z, y))
        for g in range(4)
    ]
    for copy in f_remote:
        copy.start()
    r_local.wait()
    r_remote.wait_recv()
    for s in range(2):
        for i in range(2):
            weights[s, 64 * i : 64 * i + 64, 256 * i : 256 * i + 256] = rights[s, i]
    for g in range(4):
        local[g].wait()
        f_remote[g].wait_recv()

    def left_pass(g, u, k):
        return remote(lefts.at[g, u], lefts.at[g, u], y_send.at[g * 2 + u // 4, k - 1], y_recv.at[g, u],
                      dev(xh, core, xl, z, (y + k) % 4))

    def unit_of(step):
        k = step // 2
        ys = (y + k + (k // 2) * (1 - 2 * (k % 2))) % 4
        return (step % 2) * 4 + ys

    def partial(g, u):
        at = pl.ds(pl.multiple_of(u * 64, 64), 64)
        w = t = None
        for s in range(2):
            change = jnp.dot(lefts[g, u, s], weights[s], preferred_element_type=F32)
            for i in range(2):
                f = fish[g, s, i, at, :].astype(F32)
                term = f * change[:, 256 * i : 256 * i + 256]
                w = term if w is None else w + term
                t = f if t is None else t + f
        return w, t

    def x_copy(rel, u):
        target = (x + rel) % 4
        return remote(sent.at[rel - 1, u], got.at[rel - 1, u], x_send.at[rel - 1, u], x_recv.at[rel - 1, u],
                      dev(target // 2, core, target % 2, z, y))

    def compute(step):
        u = unit_of(step)
        for rel in (2, 1, 3, 0):
            g = (x + rel) % 4

            @pl.when(step < 2)
            def _():
                for s in range(2):
                    pltpu.make_async_copy(packed, lefts.at[g, u, s], l_recv.at[g * 2 + u // 4, s]).wait()
                for k in (2, 1, 3):
                    left_pass(g, u, k).start()

            @pl.when(step >= 2)
            def _():
                left_pass(g, u, 1).wait_recv()

            w, t = partial(g, u)
            if rel:
                sent[rel - 1, u, 0] = encode(w, W_KNEE, W_SCALE)
                sent[rel - 1, u, 1] = encode_total(t)
                x_copy(rel, u).start()
            else:
                own[u, 0] = w
                own[u, 1] = t

    def d_copy(u, k):
        return remote(delta_out.at[u, k], delta_in.at[z * 4 + y], d_send.at[u, k], d_recv.at[z * 4 + y],
                      dev(xh, core, xl, u, k))

    self_copy = pltpu.make_async_copy(delta_out.at[z, y], delta_in.at[z * 4 + y], d_recv.at[z * 4 + y])

    def combine(step):
        u = unit_of(step)
        for rel in (1, 2, 3):
            x_copy(rel, u).wait_recv()
        w = own[u, 0] + decode(got[1, u, 0], W_KNEE, W_SCALE)
        t = own[u, 1] + decode_total(got[1, u, 1])
        near = encode(w / t, D_KNEE, D_SCALE)
        w = decode(got[0, u, 0], W_KNEE, W_SCALE) + decode(got[2, u, 0], W_KNEE, W_SCALE)
        t = decode_total(got[0, u, 1]) + decode_total(got[2, u, 1])
        far = encode(w / t, D_KNEE, D_SCALE)
        for k in range(4):
            delta_out[u, k, :, :256] = near[16 * k : 16 * k + 16]
            delta_out[u, k, :, 256:] = far[16 * k : 16 * k + 16]
        for k in range(4):
            here = jnp.logical_and(u == z, k == y)

            @pl.when(here)
            def _():
                self_copy.start()

            @pl.when(jnp.logical_not(here))
            def _():
                d_copy(u, k).start()

    def step_body(step, carry):
        @pl.when(step < 8)
        def _():
            compute(step)

        @pl.when(step >= LAG)
        def _():
            combine(step - LAG)

        return carry

    lax.fori_loop(0, 8 + LAG, step_body, 0)

    def finish(n, carry):
        src = (z * 4 + y + n) % 32
        pltpu.make_async_copy(delta_out.at[0, 0], delta_in.at[src], d_recv.at[src]).wait()
        for part, half in ((0, xl), (1, 1 - xl)):
            at = pl.ds(pl.multiple_of((half * 32 + src) * 256, 256), 256)
            delta = decode(delta_in[src, :, 256 * part : 256 * part + 256], D_KNEE, D_SCALE)
            out[:, at] = (base[:, at].astype(F32) + delta).astype(BF16)
        return carry

    lax.fori_loop(0, 32, finish, 0)

    @pl.when(zc != core)
    def _():
        first_remote.wait_send()

    def left_sent(k, carry):
        left_copy(k).wait_send()
        return carry

    lax.fori_loop(1, 16, left_sent, 0)
    r_remote.wait_send()
    for copy in f_remote:
        copy.wait_send()

    def sent_all(u, carry):
        for rel in (1, 2, 3):
            x_copy(rel, u).wait_send()
        for k in range(4):
            @pl.when(jnp.logical_not(jnp.logical_and(u == z, k == y)))
            def _():
                d_copy(u, k).wait_send()
        return carry

    lax.fori_loop(0, 8, sent_all, 0)

    def passed_all(n, carry):
        for k in (1, 2, 3):
            left_pass(n // 2, (n % 2) * 4 + y, k).wait_send()
        return carry

    lax.fori_loop(0, 8, passed_all, 0)


def shards(fisher, factor_left, factor_right, base_weight):
    dma = pltpu.SemaphoreType.DMA
    hbm, vmem = pl.BlockSpec(memory_space=pl.ANY), pl.BlockSpec(memory_space=pltpu.VMEM)
    return pl.pallas_call(
        kernel,
        out_shape=jax.ShapeDtypeStruct(base_weight.shape, BF16),
        in_specs=[hbm, vmem, vmem, vmem],
        out_specs=vmem,
        scratch_shapes=[
            pltpu.VMEM((64, 128), BF16),
            pltpu.VMEM((4, 8, 2, 64, 128), BF16),
            pltpu.VMEM((2, 2, 64, 256), BF16),
            pltpu.VMEM((2, 128, 512), BF16),
            pltpu.VMEM((4, 2, 2, 512, 256), BF16),
            pltpu.VMEM((3, 8, 2, 64, 256), BF16),
            pltpu.VMEM((8, 2, 64, 256), F32),
            pltpu.VMEM((3, 8, 2, 64, 256), BF16),
            pltpu.VMEM((8, 4, 16, 512), BF16),
            pltpu.VMEM((32, 16, 512), BF16),
            dma((4,)),
            dma((4,)),
            dma((4,)),
            dma((3,)),
            dma((16,)),
            dma(()),
            dma((8, 2)),
            dma((8, 3)),
            dma((4, 8)),
            dma((3, 8)),
            dma((3, 8)),
            dma((8, 4)),
            dma((32,)),
        ],
        compiler_params=pltpu.CompilerParams(collective_id=0, has_side_effects=True, vmem_limit_bytes=48 * 2**20),
    )(fisher, factor_left, factor_right, base_weight)


def solution(mesh):
    placed = (
        P("lang", None, "blk"),
        P("lang", "blk", None),
        P("lang", None, "blk"),
        P(("lang", "blk"), None),
    )
    return jax.shard_map(
        shards, mesh=mesh, in_specs=placed, out_specs=P(("lang", "blk"), None), check_vma=False
    )
```

```python
import jax
import jax.numpy as jnp
from jax import lax
from jax.experimental import pallas as pl
from jax.experimental.pallas import tpu as pltpu
from jax.sharding import PartitionSpec as P

BF16, F32 = jnp.bfloat16, jnp.float32
NZ, NY = 8, 4
MESH = pl.DeviceIdType.MESH
LAG = 3
W_KNEE, W_SCALE = 0.25, 2.0**-7.25
D_KNEE, D_SCALE = 0.01, 2.0**-7.4


def encode(v, knee, scale):
    c = jnp.abs(v) * (scale / knee) + scale
    c = c * c
    c = c * c
    c = c * c
    c = c * c
    return jnp.where(v < 0, -c, c).astype(BF16)


def root16(y):
    return jnp.exp2(jnp.log2(y) * (1.0 / 16))


def decode(y, knee, scale):
    y = y.astype(F32)
    v = root16(jnp.abs(y)) * (knee / scale) - knee
    return jnp.where(y < 0, -v, v)


def encode_total(t):
    c = t * 0.5
    c = c * c
    c = c * c
    c = c * c
    return (c * c).astype(BF16)


def decode_total(y):
    return root16(y.astype(F32)) * 2.0


def kernel(fisher, left_hbm, right, base_hbm, out, left, base, packed, lefts, rights, weights, fish, t_sent, t_own, t_got,
           w_sent, w_own, w_got, delta_out, delta_in, in_sem, f_local, f_send, f_recv, r_sem, p_send, p_recv, z_send, y_send, l_recv,
           t_send, t_recv, w_send, w_recv, d_send, d_recv, token):
    lang, blk = lax.axis_index("lang"), lax.axis_index("blk")
    xh, core = lang // 2, lang % 2
    xl, z, y = blk // 32, (blk // 4) % 8, blk % 4
    x = 2 * xh + xl
    zc, zi = z // 4, z % 4
    other = 1 - core

    def dev(xh_, c_, xl_, z_, y_):
        return {"lang": 2 * xh_ + c_, "blk": 32 * xl_ + 4 * z_ + y_}

    def remote(src, dst, send, recv, device):
        return pltpu.make_async_remote_copy(
            src_ref=src, dst_ref=dst, send_sem=send, recv_sem=recv, device_id=device, device_id_type=MESH
        )

    def signal(semaphore, device):
        pl.semaphore_signal(semaphore, inc=1, device_id=device, device_id_type=MESH)

    def in_z(n):
        return dev(xh, core, xl, (z + n) % 8, y)

    def in_y(n):
        return dev(xh, core, xl, z, (y + n) % 4)

    partner, beside = dev(xh, other, xl, z, y), dev(xh, core, 1 - xl, z, y)
    barrier = pltpu.get_barrier_semaphore()
    for device in (in_z(2), in_z(6), in_y(2), in_z(1), in_z(7), in_y(1), in_y(3), dev(1 - xh, core, xl, z, y),
                   dev(1 - xh, core, 1 - xl, z, y), beside, partner):
        signal(barrier, device)

    left_in = pltpu.make_async_copy(left_hbm, left, in_sem.at[0])
    left_in.start()

    def ranking(c):
        near, far = (228, 225, 54, 27), (27, 75, 180, 228)

        def pick(options):
            return jnp.where(zi < 2, jnp.where(zi == 0, options[0], options[1]), jnp.where(zi == 2, options[2], options[3]))

        return jnp.where(zc == c, pick(near), pick(far))

    rank, rank_other = ranking(core), ranking(other)

    def digit(word, n):
        return lax.shift_right_logical(word, 2 * n) & 3

    def rows(xs, c, zq):
        return pl.ds(pl.multiple_of(1024 * (2 * xs + c) + 256 * zq, 256), 256)

    def f_own(zq, xs):
        return pltpu.make_async_copy(fisher.at[:, rows(xs, core, zq), :], fish.at[zq, xs, core], f_local.at[zq, xs])

    def f_swap(zq, xs):
        return remote(fisher.at[:, rows(xs, other, zq), :], fish.at[zq, xs, core], f_send.at[zq, xs], f_recv.at[zq, xs], partner)

    for n in range(4):
        for xs in range(2):
            f_own(digit(rank, n), xs).start()
    r_local = pltpu.make_async_copy(right, rights.at[core], r_sem.at[0])
    r_local.start()
    base_in = pltpu.make_async_copy(base_hbm, base, in_sem.at[1])
    base_in.start()
    weights[...] = jnp.zeros_like(weights)
    left_in.wait()
    packed[...] = jnp.concatenate([left[0], left[1]], axis=1)
    pl.semaphore_wait(barrier, 11)

    signal(token.at[0], in_z(2))
    signal(token.at[0], in_z(6))
    home = zc == core
    p_local = pltpu.make_async_copy(packed, lefts.at[zi, y, core, xl], p_recv)
    p_near = remote(packed, lefts.at[zi, y, core, xl], p_send, p_recv, partner)

    @pl.when(home)
    def _():
        p_local.start()

    @pl.when(jnp.logical_not(home))
    def _():
        p_near.start()

    f_swap(digit(rank_other, 0), 0).start()
    f_swap(digit(rank_other, 0), 1).start()
    r_remote = remote(right, rights.at[core], r_sem.at[1], r_sem.at[2], partner)
    r_remote.start()
    for n in range(1, 4):
        for xs in range(2):
            f_swap(digit(rank_other, n), xs).start()

    def t_copy(g, zb):
        return remote(t_sent.at[g, zb], t_got.at[zb, (g - x + 4) % 4 - 1], t_send, t_recv, dev(g // 2, core, g % 2, z, y))

    def w_copy(g, u):
        return remote(w_sent.at[g, u], w_got.at[u, (g - x + 4) % 4 - 1], w_send, w_recv.at[u], dev(g // 2, core, g % 2, z, y))

    def totals(n, carry):
        zq, xs = digit(rank, n // 2), n % 2
        f_own(zq, xs).wait()
        pltpu.make_async_copy(fisher.at[:, rows(xs, core, zq), :], fish.at[zq, xs, other], f_recv.at[zq, xs]).wait()
        t = fish[zq, xs, 0, 0].astype(F32) + fish[zq, xs, 0, 1].astype(F32)
        t = t + (fish[zq, xs, 1, 0].astype(F32) + fish[zq, xs, 1, 1].astype(F32))
        g, zb = 2 * xs + zq // 2, zq % 2

        @pl.when(g == x)
        def _():
            t_own[zb] = t

        @pl.when(g != x)
        def _():
            t_sent[g, zb] = encode_total(t)
            t_copy(g, zb).start()

        return carry

    def spread(n, carry):
        to = dev(xh, core, (xl + n // 8) % 2, (z + n) % 8, y)
        remote(lefts.at[zi, y, :, xl], lefts.at[zi, y, :, xl], z_send, l_recv.at[zi, y], to).start()
        return carry

    lax.fori_loop(0, 2, totals, 0)
    pl.semaphore_wait(token.at[0], 2)
    signal(token.at[1], beside)

    @pl.when(home)
    def _():
        pltpu.make_async_copy(lefts.at[zi, y, :, xl], lefts.at[zi, y, :, xl], p_recv).wait()
        lax.fori_loop(1, 8, spread, 0)

    lax.fori_loop(2, 4, totals, 0)
    pl.semaphore_wait(token.at[1], 1)

    @pl.when(home)
    def _():
        lax.fori_loop(8, 16, spread, 0)

    lax.fori_loop(4, 8, totals, 0)
    r_local.wait()
    r_remote.wait_recv()
    for s in range(2):
        for i in range(2):
            weights[s, 64 * i : 64 * i + 64, 256 * i : 256 * i + 256] = rights[s, i]

    def pass_y(zq, n):
        return remote(lefts.at[zq, y], lefts.at[zq, y], y_send, l_recv.at[zq, y], in_y(n))

    def offset(k):
        return ((k + 1) % 3 + 1) * ((k + 2) // 3)

    def first_zb(ys):
        ahead = (ys - z + 8) % 8
        return jnp.where((ahead >= 2) & (ahead <= 5), 0, 1)

    def forward(n, carry):
        zq = n % 2 * 2 + (first_zb(y) + n // 2) % 2
        mine = home & (zq == zi)

        @pl.when(mine)
        def _():
            pltpu.make_async_copy(lefts.at[zq, y, :, 0], lefts.at[zq, y, :, 0], l_recv.at[zq, y]).wait()

        @pl.when(jnp.logical_not(mine))
        def _():
            pltpu.make_async_copy(lefts.at[zq, y], lefts.at[zq, y], l_recv.at[zq, y]).wait()

        pass_y(zq, 1).start()
        pass_y(zq, 3).start()
        pass_y(zq, 2).start()
        return carry

    lax.fori_loop(0, 4, forward, 0)

    def item(n, carry):
        k = n // 2 % 4
        ys = (y + offset(k)) % 4
        zq = n % 2 * 2 + (first_zb(ys) + n // 8) % 2

        @pl.when(k > 0)
        def _():
            pltpu.make_async_copy(lefts.at[zq, ys], lefts.at[zq, ys], l_recv.at[zq, ys]).wait()

        at = pl.ds(pl.multiple_of(ys * 64, 64), 64)
        u = (zq % 2) * 4 + ys
        w = None
        for s in range(2):
            lhs = lefts[zq, ys, s].reshape(128, 128)
            for i in range(2):
                change = jnp.dot(lhs, weights[s, :, 256 * i : 256 * i + 256], preferred_element_type=F32)
                term = fish[zq, :, s, i, at, :].astype(F32).reshape(128, 256) * change
                w = term if w is None else w + term
        for xs in range(2):
            g = 2 * xs + zq // 2
            half = slice(64 * xs, 64 * xs + 64)

            @pl.when(g == x)
            def _():
                w_own[u] = w[half]

            @pl.when(g != x)
            def _():
                w_sent[g, u] = encode(w[half], W_KNEE, W_SCALE)
                w_copy(g, u).start()

        return carry

    def combine(step, carry):
        ys = (y + offset(step % 4)) % 4
        zb = (first_zb(ys) + step // 4) % 2
        u = zb * 4 + ys

        @pl.when(step == 0)
        def _():
            pltpu.make_async_copy(t_got, t_got, t_recv).wait()

        pltpu.make_async_copy(w_got.at[u], w_got.at[u], w_recv.at[u]).wait()
        at = pl.ds(pl.multiple_of(ys * 64, 64), 64)
        w = w_own[u] + decode(w_got[u, 1], W_KNEE, W_SCALE)
        t = t_own[zb, at] + decode_total(t_got[zb, 1, at])
        near = encode(w / t, D_KNEE, D_SCALE)
        w = decode(w_got[u, 0], W_KNEE, W_SCALE) + decode(w_got[u, 2], W_KNEE, W_SCALE)
        t = decode_total(t_got[zb, 0, at]) + decode_total(t_got[zb, 2, at])
        far = encode(w / t, D_KNEE, D_SCALE)
        for k in range(4):
            delta_out[u, k, :, :256] = near[16 * k : 16 * k + 16]
            delta_out[u, k, :, 256:] = far[16 * k : 16 * k + 16]
        for k in range(4):
            here = jnp.logical_and(u == z, k == y)
            d_copy = remote(delta_out.at[u, k], delta_in.at[z * 4 + y], d_send, d_recv.at[z * 4 + y], dev(xh, core, xl, u, k))

            @pl.when(here)
            def _():
                pltpu.make_async_copy(delta_out.at[u, k], delta_in.at[z * 4 + y], d_recv.at[z * 4 + y]).start()

            @pl.when(jnp.logical_not(here))
            def _():
                d_copy.start()

        return carry

    def finish(n, carry):
        zs = (z + 3 + n % 4 + 4 * (n // 16)) % 8
        src = zs * 4 + (zi - offset(n // 4 % 4) + 4) % 4
        pltpu.make_async_copy(delta_out.at[0, 0], delta_in.at[src], d_recv.at[src]).wait()
        for part, half in ((0, xl), (1, 1 - xl)):
            at = pl.ds(pl.multiple_of((half * 32 + src) * 256, 256), 256)
            delta = decode(delta_in[src, :, 256 * part : 256 * part + 256], D_KNEE, D_SCALE)
            out[:, at] = (base[:, at].astype(F32) + delta).astype(BF16)
        return carry

    def unit(m, carry):
        @pl.when(m < 8)
        def _():
            lax.fori_loop(2 * m, 2 * m + 2, item, 0)

        @pl.when(m >= LAG)
        def _():
            combine(m - LAG, 0)

        return carry

    lax.fori_loop(0, 6 + LAG, unit, 0)
    base_in.wait()
    lax.fori_loop(0, 12, finish, 0)
    lax.fori_loop(6 + LAG, 8 + LAG, unit, 0)
    lax.fori_loop(12, 32, finish, 0)

    @pl.when(home)
    def _():
        pltpu.make_async_copy(delta_in.at[0:30], delta_in.at[0:30], z_send).wait()

    @pl.when(jnp.logical_not(home))
    def _():
        p_near.wait_send()

    r_remote.wait_send()
    for zq in range(4):
        for xs in range(2):
            f_swap(zq, xs).wait_send()
    for sem, view in ((y_send, lefts.at[0:3]), (t_send, t_got), (w_send, w_got), (d_send, delta_in.at[0:31])):
        pltpu.make_async_copy(view, view, sem).wait()


def shards(fisher, factor_left, factor_right, base_weight):
    dma = pltpu.SemaphoreType.DMA
    hbm, vmem = pl.BlockSpec(memory_space=pltpu.HBM), pl.BlockSpec(memory_space=pltpu.VMEM)
    return pl.pallas_call(
        kernel,
        out_shape=jax.ShapeDtypeStruct(base_weight.shape, BF16),
        in_specs=[hbm] * 4,
        out_specs=vmem,
        scratch_shapes=[
            pltpu.VMEM(factor_left.shape, BF16),
            pltpu.VMEM(base_weight.shape, BF16),
            pltpu.VMEM((64, 128), BF16),
            pltpu.VMEM((4, 4, 2, 2, 64, 128), BF16),
            pltpu.VMEM((2, 2, 64, 256), BF16),
            pltpu.VMEM((2, 128, 512), BF16),
            pltpu.VMEM((4, 2, 2, 2, 256, 256), BF16),
            pltpu.VMEM((4, 2, 256, 256), BF16),
            pltpu.VMEM((2, 256, 256), F32),
            pltpu.VMEM((2, 3, 256, 256), BF16),
            pltpu.VMEM((4, 8, 64, 256), BF16),
            pltpu.VMEM((8, 64, 256), F32),
            pltpu.VMEM((8, 3, 64, 256), BF16),
            pltpu.VMEM((8, 4, 16, 512), BF16),
            pltpu.VMEM((32, 16, 512), BF16),
            dma((2,)),
            dma((4, 2)),
            dma((4, 2)),
            dma((4, 2)),
            dma((3,)),
            dma(()),
            dma(()),
            dma(()),
            dma(()),
            dma((4, 4)),
            dma(()),
            dma(()),
            dma(()),
            dma((8,)),
            dma(()),
            dma((32,)),
            pltpu.SemaphoreType.REGULAR((2,)),
        ],
        compiler_params=pltpu.CompilerParams(collective_id=0, has_side_effects=True, vmem_limit_bytes=67043328),
    )(fisher, factor_left, factor_right, base_weight)


def solution(mesh):
    placed = (
        P("lang", None, "blk"),
        P("lang", "blk", None),
        P("lang", None, "blk"),
        P(("lang", "blk"), None),
    )
    return jax.shard_map(
        shards, mesh=mesh, in_specs=placed, out_specs=P(("lang", "blk"), None), check_vma=False
    )
```

```python
import jax
import jax.numpy as jnp
from jax import lax
from jax.experimental import pallas as pl
from jax.experimental.pallas import tpu as pltpu
from jax.sharding import PartitionSpec as P

BF16, F32 = jnp.bfloat16, jnp.float32
NZ, NY = 8, 4
MESH = pl.DeviceIdType.MESH
LAG = 3
W_KNEE, W_SCALE = 0.25, 2.0**-7.25
D_KNEE, D_SCALE = 0.01, 2.0**-7.4


def encode(v, knee, scale):
    c = jnp.abs(v) * (scale / knee) + scale
    c = c * c
    c = c * c
    c = c * c
    c = c * c
    return jnp.where(v < 0, -c, c).astype(BF16)


def root16(y):
    return jnp.exp2(jnp.log2(y) * (1.0 / 16))


def decode(y, knee, scale):
    y = y.astype(F32)
    v = root16(jnp.abs(y)) * (knee / scale) - knee
    return jnp.where(y < 0, -v, v)


def encode_total(t):
    c = t * 0.5
    c = c * c
    c = c * c
    c = c * c
    return (c * c).astype(BF16)


def decode_total(y):
    return root16(y.astype(F32)) * 2.0


def kernel(fisher, left_hbm, right, base_hbm, out, left, base, packed, lefts, rights, weights, fish, t_sent, t_own, t_got,
           w_sent, w_own, w_got, delta_out, delta_in, in_sem, f_local, f_send, f_recv, r_sem, p_send, p_recv, z_send, y_send, l_recv,
           t_send, t_recv, w_send, w_recv, d_send, d_recv, token):
    lang, blk = lax.axis_index("lang"), lax.axis_index("blk")
    xh, core = lang // 2, lang % 2
    xl, z, y = blk // 32, (blk // 4) % 8, blk % 4
    x = 2 * xh + xl
    zc, zi = z // 4, z % 4
    other = 1 - core

    def dev(xh_, c_, xl_, z_, y_):
        return {"lang": 2 * xh_ + c_, "blk": 32 * xl_ + 4 * z_ + y_}

    def remote(src, dst, send, recv, device):
        return pltpu.make_async_remote_copy(
            src_ref=src, dst_ref=dst, send_sem=send, recv_sem=recv, device_id=device, device_id_type=MESH
        )

    def signal(semaphore, device):
        pl.semaphore_signal(semaphore, inc=1, device_id=device, device_id_type=MESH)

    def in_z(n):
        return dev(xh, core, xl, (z + n) % 8, y)

    def in_y(n):
        return dev(xh, core, xl, z, (y + n) % 4)

    partner, beside = dev(xh, other, xl, z, y), dev(xh, core, 1 - xl, z, y)
    barrier = pltpu.get_barrier_semaphore()
    for device in (in_z(2), in_z(6), in_y(2), in_z(1), in_z(7), in_y(1), in_y(3), dev(1 - xh, core, xl, z, y),
                   dev(1 - xh, core, 1 - xl, z, y), beside, partner):
        signal(barrier, device)

    left_in = pltpu.make_async_copy(left_hbm, left, in_sem.at[0])
    left_in.start()

    def quarter(n):
        return n % 2 * 2 + (z + n // 2) % 2

    def rows(xs, c, zq):
        return pl.ds(pl.multiple_of(1024 * (2 * xs + c) + 256 * zq, 256), 256)

    def f_own(zq, xs):
        return pltpu.make_async_copy(fisher.at[:, rows(xs, core, zq), :], fish.at[zq, xs, core], f_local.at[zq, xs])

    def f_swap(zq, xs):
        return remote(fisher.at[:, rows(xs, other, zq), :], fish.at[zq, xs, core], f_send.at[zq, xs], f_recv.at[zq, xs], partner)

    for n in range(4):
        for xs in range(2):
            f_own(quarter(n), xs).start()
    r_local = pltpu.make_async_copy(right, rights.at[core], r_sem.at[0])
    r_local.start()
    base_in = pltpu.make_async_copy(base_hbm, base, in_sem.at[1])
    base_in.start()
    weights[...] = jnp.zeros_like(weights)
    left_in.wait()
    packed[...] = jnp.concatenate([left[0], left[1]], axis=1)
    pl.semaphore_wait(barrier, 11)

    signal(token.at[0], in_z(2))
    signal(token.at[0], in_z(6))
    home = zc == core
    p_local = pltpu.make_async_copy(packed, lefts.at[zi, y, core, xl], p_recv)
    p_near = remote(packed, lefts.at[zi, y, core, xl], p_send, p_recv, partner)

    @pl.when(home)
    def _():
        p_local.start()

    @pl.when(jnp.logical_not(home))
    def _():
        p_near.start()

    f_swap(quarter(0), 0).start()
    f_swap(quarter(0), 1).start()
    r_remote = remote(right, rights.at[core], r_sem.at[1], r_sem.at[2], partner)
    r_remote.start()
    for n in range(1, 4):
        for xs in range(2):
            f_swap(quarter(n), xs).start()

    def t_copy(g, zb):
        return remote(t_sent.at[g, zb], t_got.at[zb, (g - x + 4) % 4 - 1], t_send, t_recv.at[zb], dev(g // 2, core, g % 2, z, y))

    def w_copy(g, u):
        return remote(w_sent.at[g, u], w_got.at[u, (g - x + 4) % 4 - 1], w_send, w_recv.at[u], dev(g // 2, core, g % 2, z, y))

    def totals(n, carry):
        zq, xs = quarter(n // 2), n % 2
        f_own(zq, xs).wait()
        pltpu.make_async_copy(fisher.at[:, rows(xs, core, zq), :], fish.at[zq, xs, other], f_recv.at[zq, xs]).wait()
        t = fish[zq, xs, 0, 0].astype(F32) + fish[zq, xs, 0, 1].astype(F32)
        t = t + (fish[zq, xs, 1, 0].astype(F32) + fish[zq, xs, 1, 1].astype(F32))
        g, zb = 2 * xs + zq // 2, zq % 2

        @pl.when(g == x)
        def _():
            t_own[zb] = t

        @pl.when(g != x)
        def _():
            t_sent[g, zb] = encode_total(t)
            t_copy(g, zb).start()

        return carry

    def spread(xs, n):
        to = dev(xh, core, xs, (z + n) % 8, y)
        remote(lefts.at[zi, y, :, xl], lefts.at[zi, y, :, xl], z_send, l_recv.at[zi, y], to).start()

    pl.semaphore_wait(token.at[0], 2)
    signal(token.at[1], beside)

    @pl.when(home)
    def _():
        pltpu.make_async_copy(lefts.at[zi, y, :, xl], lefts.at[zi, y, :, xl], p_recv).wait()
        for n in (2, 6, 4):
            spread(xl, n)

    lax.fori_loop(0, 2, totals, 0)
    pl.semaphore_wait(token.at[1], 1)

    @pl.when(home)
    def _():
        for n in (0, 2, 6, 4):
            spread(1 - xl, n)
        for n in (1, 7, 3, 5):
            spread(xl, n)
            spread(1 - xl, n)

    lax.fori_loop(2, 8, totals, 0)
    r_local.wait()
    r_remote.wait_recv()
    for s in range(2):
        for i in range(2):
            weights[s, 64 * i : 64 * i + 64, 256 * i : 256 * i + 256] = rights[s, i]

    def pass_y(zq, n):
        return remote(lefts.at[zq, y], lefts.at[zq, y], y_send, l_recv.at[zq, y], in_y(n))

    def offset(k):
        return ((k + 1) % 3 + 1) * ((k + 2) // 3)

    def forward(n, carry):
        zq = quarter(n)
        mine = home & (zq == zi)

        @pl.when(mine)
        def _():
            pltpu.make_async_copy(lefts.at[zq, y, :, 0], lefts.at[zq, y, :, 0], l_recv.at[zq, y]).wait()

        @pl.when(jnp.logical_not(mine))
        def _():
            pltpu.make_async_copy(lefts.at[zq, y], lefts.at[zq, y], l_recv.at[zq, y]).wait()

        pass_y(zq, 1).start()
        pass_y(zq, 3).start()
        return carry

    lax.fori_loop(0, 4, forward, 0)

    def arrived(zq, ys):
        pltpu.make_async_copy(lefts.at[zq, ys], lefts.at[zq, ys], l_recv.at[zq, ys]).wait()

    def relay(zq, k):
        half = lefts.at[zq, (y + offset(k)) % 4, k - 1]
        remote(half, half, y_send, l_recv.at[zq, (y + offset(k)) % 4], in_y(2 * k - 1)).start()

    def relay_rest(n, carry):
        zq, k = quarter(2 + n % 2), 1 + n // 2
        arrived(zq, (y + offset(k)) % 4)
        relay(zq, k)
        return carry

    def item(n, carry):
        k = n // 2 % 4
        zq = n % 2 * 2 + (z + n // 8) % 2
        ys = (y + offset(k)) % 4

        @pl.when((k == 3) | ((k > 0) & (n < 8)))
        def _():
            arrived(zq, ys)

        @pl.when(((k == 1) | (k == 2)) & (n < 8))
        def _():
            relay(zq, k)

        at = pl.ds(pl.multiple_of(ys * 64, 64), 64)
        u = (zq % 2) * 4 + ys
        w = None
        for s in range(2):
            lhs = lefts[zq, ys, s].reshape(128, 128)
            for i in range(2):
                change = jnp.dot(lhs, weights[s, :, 256 * i : 256 * i + 256], preferred_element_type=F32)
                term = fish[zq, :, s, i, at, :].astype(F32).reshape(128, 256) * change
                w = term if w is None else w + term
        for xs in range(2):
            g = 2 * xs + zq // 2
            half = slice(64 * xs, 64 * xs + 64)

            @pl.when(g == x)
            def _():
                w_own[u] = w[half]

            @pl.when(g != x)
            def _():
                w_sent[g, u] = encode(w[half], W_KNEE, W_SCALE)
                w_copy(g, u).start()

        return carry

    def combine(step, carry):
        ys = (y + offset(step % 4)) % 4
        zb = (z + step // 4) % 2
        u = zb * 4 + ys

        @pl.when(step % 4 == 0)
        def _():
            pltpu.make_async_copy(t_got.at[zb], t_got.at[zb], t_recv.at[zb]).wait()

        pltpu.make_async_copy(w_got.at[u], w_got.at[u], w_recv.at[u]).wait()
        at = pl.ds(pl.multiple_of(ys * 64, 64), 64)
        w = w_own[u] + decode(w_got[u, 1], W_KNEE, W_SCALE)
        t = t_own[zb, at] + decode_total(t_got[zb, 1, at])
        near = encode(w / t, D_KNEE, D_SCALE)
        w = decode(w_got[u, 0], W_KNEE, W_SCALE) + decode(w_got[u, 2], W_KNEE, W_SCALE)
        t = decode_total(t_got[zb, 0, at]) + decode_total(t_got[zb, 2, at])
        far = encode(w / t, D_KNEE, D_SCALE)
        for k in range(4):
            delta_out[u, k, :, :256] = near[16 * k : 16 * k + 16]
            delta_out[u, k, :, 256:] = far[16 * k : 16 * k + 16]
        for k in range(4):
            here = jnp.logical_and(u == z, k == y)
            d_copy = remote(delta_out.at[u, k], delta_in.at[z * 4 + y], d_send, d_recv.at[z * 4 + y], dev(xh, core, xl, u, k))

            @pl.when(here)
            def _():
                pltpu.make_async_copy(delta_out.at[u, k], delta_in.at[z * 4 + y], d_recv.at[z * 4 + y]).start()

            @pl.when(jnp.logical_not(here))
            def _():
                d_copy.start()

        return carry

    def finish(n, carry):
        zs = 2 * ((n + z // 2) % 4) + (zc + n // 16) % 2
        src = zs * 4 + (zi - offset(n // 4 % 4) + 4) % 4
        pltpu.make_async_copy(delta_out.at[0, 0], delta_in.at[src], d_recv.at[src]).wait()
        for part, half in ((0, xl), (1, 1 - xl)):
            at = pl.ds(pl.multiple_of((half * 32 + src) * 256, 256), 256)
            delta = decode(delta_in[src, :, 256 * part : 256 * part + 256], D_KNEE, D_SCALE)
            out[:, at] = (base[:, at].astype(F32) + delta).astype(BF16)
        return carry

    def unit(m, carry):
        @pl.when(m < 8)
        def _():
            lax.fori_loop(2 * m, 2 * m + 2, item, 0)

        @pl.when(m == 3)
        def _():
            lax.fori_loop(0, 4, relay_rest, 0)

        @pl.when(m >= LAG)
        def _():
            combine(m - LAG, 0)

        return carry

    lax.fori_loop(0, 6 + LAG, unit, 0)
    base_in.wait()
    lax.fori_loop(0, 12, finish, 0)
    lax.fori_loop(6 + LAG, 8 + LAG, unit, 0)
    lax.fori_loop(12, 32, finish, 0)

    @pl.when(home)
    def _():
        pltpu.make_async_copy(delta_in.at[0:30], delta_in.at[0:30], z_send).wait()

    @pl.when(jnp.logical_not(home))
    def _():
        p_near.wait_send()

    r_remote.wait_send()
    for zq in range(4):
        for xs in range(2):
            f_swap(zq, xs).wait_send()
    for sem, view in ((y_send, lefts.at[0:3]), (t_send, t_got), (w_send, w_got), (d_send, delta_in.at[0:31])):
        pltpu.make_async_copy(view, view, sem).wait()


def shards(fisher, factor_left, factor_right, base_weight):
    dma = pltpu.SemaphoreType.DMA
    hbm, vmem = pl.BlockSpec(memory_space=pltpu.HBM), pl.BlockSpec(memory_space=pltpu.VMEM)
    return pl.pallas_call(
        kernel,
        out_shape=jax.ShapeDtypeStruct(base_weight.shape, BF16),
        in_specs=[hbm] * 4,
        out_specs=vmem,
        scratch_shapes=[
            pltpu.VMEM(factor_left.shape, BF16),
            pltpu.VMEM(base_weight.shape, BF16),
            pltpu.VMEM((64, 128), BF16),
            pltpu.VMEM((4, 4, 2, 2, 64, 128), BF16),
            pltpu.VMEM((2, 2, 64, 256), BF16),
            pltpu.VMEM((2, 128, 512), BF16),
            pltpu.VMEM((4, 2, 2, 2, 256, 256), BF16),
            pltpu.VMEM((4, 2, 256, 256), BF16),
            pltpu.VMEM((2, 256, 256), F32),
            pltpu.VMEM((2, 3, 256, 256), BF16),
            pltpu.VMEM((4, 8, 64, 256), BF16),
            pltpu.VMEM((8, 64, 256), F32),
            pltpu.VMEM((8, 3, 64, 256), BF16),
            pltpu.VMEM((8, 4, 16, 512), BF16),
            pltpu.VMEM((32, 16, 512), BF16),
            dma((2,)),
            dma((4, 2)),
            dma((4, 2)),
            dma((4, 2)),
            dma((3,)),
            dma(()),
            dma(()),
            dma(()),
            dma(()),
            dma((4, 4)),
            dma(()),
            dma((2,)),
            dma(()),
            dma((8,)),
            dma(()),
            dma((32,)),
            pltpu.SemaphoreType.REGULAR((2,)),
        ],
        compiler_params=pltpu.CompilerParams(collective_id=0, has_side_effects=True, vmem_limit_bytes=50331648),
    )(*(pltpu.with_memory_space_constraint(a, pltpu.HBM) for a in (fisher, factor_left, factor_right, base_weight)))


def solution(mesh):
    placed = (
        P("lang", None, "blk"),
        P("lang", "blk", None),
        P("lang", None, "blk"),
        P(("lang", "blk"), None),
    )
    return jax.shard_map(
        shards, mesh=mesh, in_specs=placed, out_specs=P(("lang", "blk"), None), check_vma=False
    )
```

```python
import jax
import jax.numpy as jnp
from jax import lax
from jax.experimental import pallas as pl
from jax.experimental.pallas import tpu as pltpu
from jax.sharding import PartitionSpec as P

BF16, F32 = jnp.bfloat16, jnp.float32
NZ, NY = 8, 4
MESH = pl.DeviceIdType.MESH
LAG = 3
W_KNEE, W_SCALE = 0.25, 2.0**-7.25
D_KNEE, D_SCALE = 0.01, 2.0**-7.4


def encode(v, knee, scale):
    c = jnp.abs(v) * (scale / knee) + scale
    c = c * c
    c = c * c
    c = c * c
    c = c * c
    return jnp.where(v < 0, -c, c).astype(BF16)


def root16(y):
    return jnp.exp2(jnp.log2(y) * (1.0 / 16))


def decode(y, knee, scale):
    y = y.astype(F32)
    v = root16(jnp.abs(y)) * (knee / scale) - knee
    return jnp.where(y < 0, -v, v)


def encode_total(t):
    c = t * 0.5
    c = c * c
    c = c * c
    c = c * c
    return (c * c).astype(BF16)


def decode_total(y):
    return root16(y.astype(F32)) * 2.0


def kernel(fisher, left_hbm, right, base_hbm, out, left, base, packed, lefts, rights, weights, fish, t_sent, t_own, t_got,
           w_sent, w_own, w_got, delta_out, delta_in, in_sem, f_local, f_send, f_recv, r_sem, p_send, p_recv, z_send, y_send, l_recv,
           t_send, t_recv, w_send, w_recv, d_send, d_recv, token):
    lang, blk = lax.axis_index("lang"), lax.axis_index("blk")
    xh, core = lang // 2, lang % 2
    xl, z, y = blk // 32, (blk // 4) % 8, blk % 4
    x = 2 * xh + xl
    zc, zi = z // 4, z % 4
    other = 1 - core

    def dev(xh_, c_, xl_, z_, y_):
        return {"lang": 2 * xh_ + c_, "blk": 32 * xl_ + 4 * z_ + y_}

    def remote(src, dst, send, recv, device):
        return pltpu.make_async_remote_copy(
            src_ref=src, dst_ref=dst, send_sem=send, recv_sem=recv, device_id=device, device_id_type=MESH
        )

    def signal(semaphore, device):
        pl.semaphore_signal(semaphore, inc=1, device_id=device, device_id_type=MESH)

    def in_z(n):
        return dev(xh, core, xl, (z + n) % 8, y)

    def in_y(n):
        return dev(xh, core, xl, z, (y + n) % 4)

    partner, beside = dev(xh, other, xl, z, y), dev(xh, core, 1 - xl, z, y)
    left_in = pltpu.make_async_copy(left_hbm, left, in_sem.at[0])
    left_in.start()
    barrier = pltpu.get_barrier_semaphore()
    for device in (in_z(2), in_z(6), in_y(2), in_z(1), in_z(7), in_y(1), in_y(3), dev(1 - xh, core, xl, z, y),
                   dev(1 - xh, core, 1 - xl, z, y), beside, partner):
        signal(barrier, device)


    def quarter(n):
        return n % 2 * 2 + (z + n // 2) % 2

    def rows(xs, c, zq):
        return pl.ds(pl.multiple_of(1024 * (2 * xs + c) + 256 * zq, 256), 256)

    def f_own(zq, xs):
        return pltpu.make_async_copy(fisher.at[:, rows(xs, core, zq), :], fish.at[zq, xs, core], f_local.at[zq, xs])

    def f_swap(zq, xs):
        return remote(fisher.at[:, rows(xs, other, zq), :], fish.at[zq, xs, core], f_send.at[zq, xs], f_recv.at[zq, xs], partner)

    for n in range(4):
        for xs in range(2):
            f_own(quarter(n), xs).start()
    r_local = pltpu.make_async_copy(right, rights.at[core], r_sem.at[0])
    r_local.start()
    base_in = pltpu.make_async_copy(base_hbm, base, in_sem.at[1])
    base_in.start()
    weights[...] = jnp.zeros_like(weights)
    pl.semaphore_wait(barrier, 11)
    f_swap(quarter(0), 0).start()
    left_in.wait()
    packed[...] = jnp.concatenate([left[0], left[1]], axis=1)

    signal(token.at[0], in_z(2))
    signal(token.at[0], in_z(6))
    home = zc == core
    p_local = pltpu.make_async_copy(packed, lefts.at[zi, y, core, xl], p_recv)
    p_near = remote(packed, lefts.at[zi, y, core, xl], p_send, p_recv, partner)

    @pl.when(home)
    def _():
        p_local.start()

    @pl.when(jnp.logical_not(home))
    def _():
        p_near.start()

    f_swap(quarter(0), 1).start()
    r_remote = remote(right, rights.at[core], r_sem.at[1], r_sem.at[2], partner)
    r_remote.start()
    for n in range(1, 4):
        for xs in range(2):
            f_swap(quarter(n), xs).start()

    def t_copy(g, zb):
        return remote(t_sent.at[g, zb], t_got.at[zb, (g - x + 4) % 4 - 1], t_send, t_recv.at[zb], dev(g // 2, core, g % 2, z, y))

    def w_copy(g, u):
        return remote(w_sent.at[g, u], w_got.at[u, (g - x + 4) % 4 - 1], w_send, w_recv.at[u], dev(g // 2, core, g % 2, z, y))

    def totals(n, carry):
        zq, xs = quarter(n // 2), n % 2
        f_own(zq, xs).wait()
        pltpu.make_async_copy(fisher.at[:, rows(xs, core, zq), :], fish.at[zq, xs, other], f_recv.at[zq, xs]).wait()
        t = fish[zq, xs, 0, 0].astype(F32) + fish[zq, xs, 0, 1].astype(F32)
        t = t + (fish[zq, xs, 1, 0].astype(F32) + fish[zq, xs, 1, 1].astype(F32))
        g, zb = 2 * xs + zq // 2, zq % 2

        @pl.when(g == x)
        def _():
            t_own[zb] = t

        @pl.when(g != x)
        def _():
            t_sent[g, zb] = encode_total(t)
            t_copy(g, zb).start()

        return carry

    def spread(xs, n):
        to = dev(xh, core, xs, (z + n) % 8, y)
        remote(lefts.at[zi, y, :, xl], lefts.at[zi, y, :, xl], z_send, l_recv.at[zi, y], to).start()

    pl.semaphore_wait(token.at[0], 2)
    signal(token.at[1], beside)

    @pl.when(home)
    def _():
        pltpu.make_async_copy(lefts.at[zi, y, :, xl], lefts.at[zi, y, :, xl], p_recv).wait()
        for n in (2, 6, 4):
            spread(xl, n)

    lax.fori_loop(0, 2, totals, 0)
    pl.semaphore_wait(token.at[1], 1)

    @pl.when(home)
    def _():
        for n in (0, 2, 6, 4):
            spread(1 - xl, n)
        for n in (1, 7, 3, 5):
            spread(xl, n)
            spread(1 - xl, n)

    lax.fori_loop(2, 8, totals, 0)
    r_local.wait()
    r_remote.wait_recv()
    for s in range(2):
        for i in range(2):
            weights[s, 64 * i : 64 * i + 64, 256 * i : 256 * i + 256] = rights[s, i]

    def pass_y(zq, n):
        return remote(lefts.at[zq, y], lefts.at[zq, y], y_send, l_recv.at[zq, y], in_y(n))

    def offset(k):
        return ((k + 1) % 3 + 1) * ((k + 2) // 3)

    def forward(n, carry):
        zq = quarter(n)
        mine = home & (zq == zi)

        @pl.when(mine)
        def _():
            pltpu.make_async_copy(lefts.at[zq, y, :, 0], lefts.at[zq, y, :, 0], l_recv.at[zq, y]).wait()

        @pl.when(jnp.logical_not(mine))
        def _():
            pltpu.make_async_copy(lefts.at[zq, y], lefts.at[zq, y], l_recv.at[zq, y]).wait()

        pass_y(zq, 1).start()
        pass_y(zq, 3).start()
        return carry

    lax.fori_loop(0, 4, forward, 0)

    def arrived(zq, ys):
        pltpu.make_async_copy(lefts.at[zq, ys], lefts.at[zq, ys], l_recv.at[zq, ys]).wait()

    def relay(zq, k):
        half = lefts.at[zq, (y + offset(k)) % 4, k - 1]
        remote(half, half, y_send, l_recv.at[zq, (y + offset(k)) % 4], in_y(2 * k - 1)).start()

    def relay_rest(n, carry):
        zq, k = quarter(2 + n % 2), 1 + n // 2
        arrived(zq, (y + offset(k)) % 4)
        relay(zq, k)
        return carry

    def item(n, carry):
        k = n // 2 % 4
        zq = n % 2 * 2 + (z + n // 8) % 2
        ys = (y + offset(k)) % 4

        @pl.when((k == 3) | ((k > 0) & (n < 8)))
        def _():
            arrived(zq, ys)

        @pl.when(((k == 1) | (k == 2)) & (n < 8))
        def _():
            relay(zq, k)

        at = pl.ds(pl.multiple_of(ys * 64, 64), 64)
        u = (zq % 2) * 4 + ys
        w = None
        for s in range(2):
            lhs = lefts[zq, ys, s].reshape(128, 128)
            for i in range(2):
                change = jnp.dot(lhs, weights[s, :, 256 * i : 256 * i + 256], preferred_element_type=F32)
                term = fish[zq, :, s, i, at, :].astype(F32).reshape(128, 256) * change
                w = term if w is None else w + term
        for xs in range(2):
            g = 2 * xs + zq // 2
            half = slice(64 * xs, 64 * xs + 64)

            @pl.when(g == x)
            def _():
                w_own[u] = w[half]

            @pl.when(g != x)
            def _():
                w_sent[g, u] = encode(w[half], W_KNEE, W_SCALE)
                w_copy(g, u).start()

        return carry

    def combine(step, carry):
        ys = (y + offset(step % 4)) % 4
        zb = (z + step // 4) % 2
        u = zb * 4 + ys

        @pl.when(step % 4 == 0)
        def _():
            pltpu.make_async_copy(t_got.at[zb], t_got.at[zb], t_recv.at[zb]).wait()

        pltpu.make_async_copy(w_got.at[u], w_got.at[u], w_recv.at[u]).wait()
        at = pl.ds(pl.multiple_of(ys * 64, 64), 64)
        w = w_own[u] + decode(w_got[u, 1], W_KNEE, W_SCALE)
        t = t_own[zb, at] + decode_total(t_got[zb, 1, at])
        near = encode(w / t, D_KNEE, D_SCALE)
        w = decode(w_got[u, 0], W_KNEE, W_SCALE) + decode(w_got[u, 2], W_KNEE, W_SCALE)
        t = decode_total(t_got[zb, 0, at]) + decode_total(t_got[zb, 2, at])
        far = encode(w / t, D_KNEE, D_SCALE)
        for k in range(4):
            delta_out[u, k, :, :256] = near[16 * k : 16 * k + 16]
            delta_out[u, k, :, 256:] = far[16 * k : 16 * k + 16]
        for n in (2, 1, 3, 0):
            k = (y + n) % 4
            here = jnp.logical_and(u == z, k == y)
            d_copy = remote(delta_out.at[u, k], delta_in.at[z * 4 + y], d_send, d_recv.at[z * 4 + y], dev(xh, core, xl, u, k))

            @pl.when(here)
            def _():
                pltpu.make_async_copy(delta_out.at[u, k], delta_in.at[z * 4 + y], d_recv.at[z * 4 + y]).start()

            @pl.when(jnp.logical_not(here))
            def _():
                d_copy.start()

        return carry

    def finish(n, carry):
        zs = 2 * ((n + z // 2) % 4) + (zc + n // 16) % 2
        src = zs * 4 + (zi - offset(n // 4 % 4) + 4) % 4
        pltpu.make_async_copy(delta_out.at[0, 0], delta_in.at[src], d_recv.at[src]).wait()
        for part, half in ((0, xl), (1, 1 - xl)):
            at = pl.ds(pl.multiple_of((half * 32 + src) * 256, 256), 256)
            delta = decode(delta_in[src, :, 256 * part : 256 * part + 256], D_KNEE, D_SCALE)
            out[:, at] = (base[:, at].astype(F32) + delta).astype(BF16)
        return carry

    def unit(m, carry):
        @pl.when(m < 8)
        def _():
            lax.fori_loop(2 * m, 2 * m + 2, item, 0)

        @pl.when(m == 3)
        def _():
            lax.fori_loop(0, 4, relay_rest, 0)

        @pl.when(m >= LAG)
        def _():
            combine(m - LAG, 0)

        return carry

    lax.fori_loop(0, 6 + LAG, unit, 0)
    base_in.wait()
    lax.fori_loop(0, 12, finish, 0)
    lax.fori_loop(6 + LAG, 8 + LAG, unit, 0)
    lax.fori_loop(12, 32, finish, 0)

    @pl.when(home)
    def _():
        pltpu.make_async_copy(delta_in.at[0:30], delta_in.at[0:30], z_send).wait()

    @pl.when(jnp.logical_not(home))
    def _():
        p_near.wait_send()

    r_remote.wait_send()
    for zq in range(4):
        for xs in range(2):
            f_swap(zq, xs).wait_send()
    for sem, view in ((y_send, lefts.at[0:3]), (t_send, t_got), (w_send, w_got), (d_send, delta_in.at[0:31])):
        pltpu.make_async_copy(view, view, sem).wait()


def shards(fisher, factor_left, factor_right, base_weight):
    dma = pltpu.SemaphoreType.DMA
    hbm, vmem = pl.BlockSpec(memory_space=pltpu.HBM), pl.BlockSpec(memory_space=pltpu.VMEM)
    return pl.pallas_call(
        kernel,
        out_shape=jax.ShapeDtypeStruct(base_weight.shape, BF16),
        in_specs=[hbm] * 4,
        out_specs=vmem,
        scratch_shapes=[
            pltpu.VMEM(factor_left.shape, BF16),
            pltpu.VMEM(base_weight.shape, BF16),
            pltpu.VMEM((64, 128), BF16),
            pltpu.VMEM((4, 4, 2, 2, 64, 128), BF16),
            pltpu.VMEM((2, 2, 64, 256), BF16),
            pltpu.VMEM((2, 128, 512), BF16),
            pltpu.VMEM((4, 2, 2, 2, 256, 256), BF16),
            pltpu.VMEM((4, 2, 256, 256), BF16),
            pltpu.VMEM((2, 256, 256), F32),
            pltpu.VMEM((2, 3, 256, 256), BF16),
            pltpu.VMEM((4, 8, 64, 256), BF16),
            pltpu.VMEM((8, 64, 256), F32),
            pltpu.VMEM((8, 3, 64, 256), BF16),
            pltpu.VMEM((8, 4, 16, 512), BF16),
            pltpu.VMEM((32, 16, 512), BF16),
            dma((2,)),
            dma((4, 2)),
            dma((4, 2)),
            dma((4, 2)),
            dma((3,)),
            dma(()),
            dma(()),
            dma(()),
            dma(()),
            dma((4, 4)),
            dma(()),
            dma((2,)),
            dma(()),
            dma((8,)),
            dma(()),
            dma((32,)),
            pltpu.SemaphoreType.REGULAR((2,)),
        ],
        compiler_params=pltpu.CompilerParams(collective_id=0, has_side_effects=True, vmem_limit_bytes=50331648),
    )(*(pltpu.with_memory_space_constraint(a, pltpu.HBM) for a in (fisher, factor_left, factor_right, base_weight)))


def solution(mesh):
    placed = (
        P("lang", None, "blk"),
        P("lang", "blk", None),
        P("lang", None, "blk"),
        P(("lang", "blk"), None),
    )
    return jax.shard_map(
        shards, mesh=mesh, in_specs=placed, out_specs=P(("lang", "blk"), None), check_vma=False
    )
```

```python
import jax
import jax.numpy as jnp
from jax import lax
from jax.experimental import pallas as pl
from jax.experimental.pallas import tpu as pltpu
from jax.sharding import PartitionSpec as P

BF16, F32 = jnp.bfloat16, jnp.float32
NZ, NY = 8, 4
MESH = pl.DeviceIdType.MESH
LAG = 4
W_KNEE, W_SCALE = 0.25, 2.0**-7.25
D_KNEE, D_SCALE = 0.01, 2.0**-7.4


def encode(v, knee, scale):
    c = jnp.abs(v) * (scale / knee) + scale
    c = c * c
    c = c * c
    c = c * c
    c = c * c
    return jnp.where(v < 0, -c, c).astype(BF16)


def root16(y):
    return jnp.exp2(jnp.log2(y) * (1.0 / 16))


def decode(y, knee, scale):
    y = y.astype(F32)
    v = root16(jnp.abs(y)) * (knee / scale) - knee
    return jnp.where(y < 0, -v, v)


def encode_total(t):
    c = t * 0.5
    c = c * c
    c = c * c
    c = c * c
    return (c * c).astype(BF16)


def decode_total(y):
    return root16(y.astype(F32)) * 2.0


def kernel(fisher, left_hbm, right, base_hbm, out, left, base, packed, lefts, rights, weights, fish, t_sent, t_own, t_got,
           w_sent, w_own, w_got, delta_out, delta_in, in_sem, f_local, f_send, f_recv, r_sem, p_send, p_recv, z_send, y_send, l_recv,
           t_send, t_recv, w_send, w_recv, d_send, d_recv, token):
    lang, blk = lax.axis_index("lang"), lax.axis_index("blk")
    xh, core = lang // 2, lang % 2
    xl, z, y = blk // 32, (blk // 4) % 8, blk % 4
    x = 2 * xh + xl
    zc, zi = z // 4, z % 4
    other = 1 - core

    def dev(xh_, c_, xl_, z_, y_):
        return {"lang": 2 * xh_ + c_, "blk": 32 * xl_ + 4 * z_ + y_}

    def remote(src, dst, send, recv, device):
        return pltpu.make_async_remote_copy(
            src_ref=src, dst_ref=dst, send_sem=send, recv_sem=recv, device_id=device, device_id_type=MESH
        )

    def signal(semaphore, device):
        pl.semaphore_signal(semaphore, inc=1, device_id=device, device_id_type=MESH)

    def in_z(n):
        return dev(xh, core, xl, (z + n) % 8, y)

    def in_y(n):
        return dev(xh, core, xl, z, (y + n) % 4)

    partner, beside = dev(xh, other, xl, z, y), dev(xh, core, 1 - xl, z, y)
    left_in = pltpu.make_async_copy(left_hbm, left, in_sem.at[0])
    left_in.start()
    barrier = pltpu.get_barrier_semaphore()
    for device in (in_z(2), in_z(6), in_y(2), in_z(1), in_z(7), in_y(1), in_y(3), dev(1 - xh, core, xl, z, y),
                   dev(1 - xh, core, 1 - xl, z, y), beside, partner):
        signal(barrier, device)


    def quarter(n):
        return n % 2 * 2 + (z + n // 2) % 2

    def rows(xs, c, zq):
        return pl.ds(pl.multiple_of(1024 * (2 * xs + c) + 256 * zq, 256), 256)

    def f_own(zq, xs):
        return pltpu.make_async_copy(fisher.at[:, rows(xs, core, zq), :], fish.at[zq, xs, core], f_local.at[zq, xs])

    def f_swap(zq, xs):
        return remote(fisher.at[:, rows(xs, other, zq), :], fish.at[zq, xs, core], f_send.at[zq, xs], f_recv.at[zq, xs], partner)

    for n in range(4):
        for xs in range(2):
            f_own(quarter(n), xs).start()
    r_local = pltpu.make_async_copy(right, rights.at[core], r_sem.at[0])
    r_local.start()
    base_in = pltpu.make_async_copy(base_hbm, base, in_sem.at[1])
    base_in.start()
    weights[...] = jnp.zeros_like(weights)
    pl.semaphore_wait(barrier, 11)
    f_swap(quarter(0), 0).start()
    left_in.wait()
    packed[...] = jnp.concatenate([left[0], left[1]], axis=1)

    signal(token.at[0], in_z(2))
    signal(token.at[0], in_z(6))
    home = zc == core
    p_local = pltpu.make_async_copy(packed, lefts.at[zi, y, core, xl], p_recv)
    p_near = remote(packed, lefts.at[zi, y, core, xl], p_send, p_recv, partner)

    @pl.when(home)
    def _():
        p_local.start()

    @pl.when(jnp.logical_not(home))
    def _():
        p_near.start()

    f_swap(quarter(0), 1).start()
    r_remote = remote(right, rights.at[core], r_sem.at[1], r_sem.at[2], partner)
    r_remote.start()
    for n in range(1, 4):
        for xs in range(2):
            f_swap(quarter(n), xs).start()

    def t_copy(g, zb):
        return remote(t_sent.at[g, zb], t_got.at[zb, (g - x + 4) % 4 - 1], t_send, t_recv.at[zb], dev(g // 2, core, g % 2, z, y))

    def w_copy(g, u):
        return remote(w_sent.at[g, u], w_got.at[u, (g - x + 4) % 4 - 1], w_send, w_recv.at[u], dev(g // 2, core, g % 2, z, y))

    def totals(n, carry):
        zq, xs = quarter(n // 2), n % 2
        f_own(zq, xs).wait()
        pltpu.make_async_copy(fisher.at[:, rows(xs, core, zq), :], fish.at[zq, xs, other], f_recv.at[zq, xs]).wait()
        t = fish[zq, xs, 0, 0].astype(F32) + fish[zq, xs, 0, 1].astype(F32)
        t = t + (fish[zq, xs, 1, 0].astype(F32) + fish[zq, xs, 1, 1].astype(F32))
        g, zb = 2 * xs + zq // 2, zq % 2

        @pl.when(g == x)
        def _():
            t_own[zb] = t

        @pl.when(g != x)
        def _():
            t_sent[g, zb] = encode_total(t)
            t_copy(g, zb).start()

        return carry

    def spread(xs, n):
        to = dev(xh, core, xs, (z + n) % 8, y)
        remote(lefts.at[zi, y, :, xl], lefts.at[zi, y, :, xl], z_send, l_recv.at[zi, y], to).start()

    pl.semaphore_wait(token.at[0], 2)
    signal(token.at[1], beside)

    @pl.when(home)
    def _():
        pltpu.make_async_copy(lefts.at[zi, y, :, xl], lefts.at[zi, y, :, xl], p_recv).wait()
        for n in (2, 6, 4):
            spread(xl, n)

    lax.fori_loop(0, 2, totals, 0)
    pl.semaphore_wait(token.at[1], 1)

    @pl.when(home)
    def _():
        for n in (0, 2, 6, 4):
            spread(1 - xl, n)
        for n in (1, 7, 3, 5):
            spread(xl, n)
            spread(1 - xl, n)

    lax.fori_loop(2, 8, totals, 0)
    r_local.wait()
    r_remote.wait_recv()
    for s in range(2):
        for i in range(2):
            weights[s, 64 * i : 64 * i + 64, 256 * i : 256 * i + 256] = rights[s, i]

    def pass_y(zq, n):
        return remote(lefts.at[zq, y], lefts.at[zq, y], y_send, l_recv.at[zq, y], in_y(n))

    def offset(k):
        return ((k + 1) % 3 + 1) * ((k + 2) // 3)

    def forward(n, carry):
        zq = quarter(n)
        mine = home & (zq == zi)

        @pl.when(mine)
        def _():
            pltpu.make_async_copy(lefts.at[zq, y, :, 0], lefts.at[zq, y, :, 0], l_recv.at[zq, y]).wait()

        @pl.when(jnp.logical_not(mine))
        def _():
            pltpu.make_async_copy(lefts.at[zq, y], lefts.at[zq, y], l_recv.at[zq, y]).wait()

        pass_y(zq, 1).start()
        pass_y(zq, 3).start()
        return carry

    lax.fori_loop(0, 4, forward, 0)

    def arrived(zq, ys):
        pltpu.make_async_copy(lefts.at[zq, ys], lefts.at[zq, ys], l_recv.at[zq, ys]).wait()

    def relay(zq, k):
        half = lefts.at[zq, (y + offset(k)) % 4, k - 1]
        remote(half, half, y_send, l_recv.at[zq, (y + offset(k)) % 4], in_y(2 * k - 1)).start()

    def relay_rest(n, carry):
        zq, k = quarter(2 + n % 2), 1 + n // 2
        arrived(zq, (y + offset(k)) % 4)
        relay(zq, k)
        return carry

    def item(n, carry):
        k = n // 2 % 4
        zq = n % 2 * 2 + (z + n // 8) % 2
        ys = (y + offset(k)) % 4

        @pl.when((k == 3) | ((k > 0) & (n < 8)))
        def _():
            arrived(zq, ys)

        @pl.when(((k == 1) | (k == 2)) & (n < 8))
        def _():
            relay(zq, k)

        at = pl.ds(pl.multiple_of(ys * 64, 64), 64)
        u = (zq % 2) * 4 + ys
        w = None
        for s in range(2):
            lhs = lefts[zq, ys, s].reshape(128, 128)
            for i in range(2):
                change = jnp.dot(lhs, weights[s, :, 256 * i : 256 * i + 256], preferred_element_type=F32)
                term = fish[zq, :, s, i, at, :].astype(F32).reshape(128, 256) * change
                w = term if w is None else w + term
        for xs in range(2):
            g = 2 * xs + zq // 2
            half = slice(64 * xs, 64 * xs + 64)

            @pl.when(g == x)
            def _():
                w_own[u] = w[half]

            @pl.when(g != x)
            def _():
                w_sent[g, u] = encode(w[half], W_KNEE, W_SCALE)
                w_copy(g, u).start()

        return carry

    def combine(step, carry):
        ys = (y + offset(step % 4)) % 4
        zb = (z + step // 4) % 2
        u = zb * 4 + ys

        @pl.when(step % 4 == 0)
        def _():
            pltpu.make_async_copy(t_got.at[zb], t_got.at[zb], t_recv.at[zb]).wait()

        pltpu.make_async_copy(w_got.at[u], w_got.at[u], w_recv.at[u]).wait()
        at = pl.ds(pl.multiple_of(ys * 64, 64), 64)
        w = w_own[u] + decode(w_got[u, 1], W_KNEE, W_SCALE)
        t = t_own[zb, at] + decode_total(t_got[zb, 1, at])
        near = encode(w / t, D_KNEE, D_SCALE)
        w = decode(w_got[u, 0], W_KNEE, W_SCALE) + decode(w_got[u, 2], W_KNEE, W_SCALE)
        t = decode_total(t_got[zb, 0, at]) + decode_total(t_got[zb, 2, at])
        far = encode(w / t, D_KNEE, D_SCALE)
        for k in range(4):
            delta_out[u, k, :, :256] = near[16 * k : 16 * k + 16]
            delta_out[u, k, :, 256:] = far[16 * k : 16 * k + 16]
        for n in (2, 1, 3, 0):
            k = (y + n) % 4
            here = jnp.logical_and(u == z, k == y)
            d_copy = remote(delta_out.at[u, k], delta_in.at[z * 4 + y], d_send, d_recv.at[z * 4 + y], dev(xh, core, xl, u, k))

            @pl.when(here)
            def _():
                pltpu.make_async_copy(delta_out.at[u, k], delta_in.at[z * 4 + y], d_recv.at[z * 4 + y]).start()

            @pl.when(jnp.logical_not(here))
            def _():
                d_copy.start()

        return carry

    def finish(n, carry):
        zs = 2 * ((n + z // 2) % 4) + (zc + n // 16) % 2
        src = zs * 4 + (zi - offset(n // 4 % 4) + 4) % 4
        pltpu.make_async_copy(delta_out.at[0, 0], delta_in.at[src], d_recv.at[src]).wait()
        for part, half in ((0, xl), (1, 1 - xl)):
            at = pl.ds(pl.multiple_of((half * 32 + src) * 256, 256), 256)
            delta = decode(delta_in[src, :, 256 * part : 256 * part + 256], D_KNEE, D_SCALE)
            out[:, at] = (base[:, at].astype(F32) + delta).astype(BF16)
        return carry

    def unit(m, carry):
        @pl.when(m < 8)
        def _():
            lax.fori_loop(2 * m, 2 * m + 2, item, 0)

        @pl.when(m == 3)
        def _():
            lax.fori_loop(0, 4, relay_rest, 0)

        @pl.when(m >= LAG)
        def _():
            combine(m - LAG, 0)

        return carry

    lax.fori_loop(0, 6 + LAG, unit, 0)
    base_in.wait()
    lax.fori_loop(0, 12, finish, 0)
    lax.fori_loop(6 + LAG, 8 + LAG, unit, 0)
    lax.fori_loop(12, 32, finish, 0)

    @pl.when(home)
    def _():
        pltpu.make_async_copy(delta_in.at[0:30], delta_in.at[0:30], z_send).wait()

    @pl.when(jnp.logical_not(home))
    def _():
        p_near.wait_send()

    r_remote.wait_send()
    for zq in range(4):
        for xs in range(2):
            f_swap(zq, xs).wait_send()
    for sem, view in ((y_send, lefts.at[0:3]), (t_send, t_got), (w_send, w_got), (d_send, delta_in.at[0:31])):
        pltpu.make_async_copy(view, view, sem).wait()


def shards(fisher, factor_left, factor_right, base_weight):
    dma = pltpu.SemaphoreType.DMA
    hbm, vmem = pl.BlockSpec(memory_space=pltpu.HBM), pl.BlockSpec(memory_space=pltpu.VMEM)
    return pl.pallas_call(
        kernel,
        out_shape=jax.ShapeDtypeStruct(base_weight.shape, BF16),
        in_specs=[hbm] * 4,
        out_specs=vmem,
        scratch_shapes=[
            pltpu.VMEM(factor_left.shape, BF16),
            pltpu.VMEM(base_weight.shape, BF16),
            pltpu.VMEM((64, 128), BF16),
            pltpu.VMEM((4, 4, 2, 2, 64, 128), BF16),
            pltpu.VMEM((2, 2, 64, 256), BF16),
            pltpu.VMEM((2, 128, 512), BF16),
            pltpu.VMEM((4, 2, 2, 2, 256, 256), BF16),
            pltpu.VMEM((4, 2, 256, 256), BF16),
            pltpu.VMEM((2, 256, 256), F32),
            pltpu.VMEM((2, 3, 256, 256), BF16),
            pltpu.VMEM((4, 8, 64, 256), BF16),
            pltpu.VMEM((8, 64, 256), F32),
            pltpu.VMEM((8, 3, 64, 256), BF16),
            pltpu.VMEM((8, 4, 16, 512), BF16),
            pltpu.VMEM((32, 16, 512), BF16),
            dma((2,)),
            dma((4, 2)),
            dma((4, 2)),
            dma((4, 2)),
            dma((3,)),
            dma(()),
            dma(()),
            dma(()),
            dma(()),
            dma((4, 4)),
            dma(()),
            dma((2,)),
            dma(()),
            dma((8,)),
            dma(()),
            dma((32,)),
            pltpu.SemaphoreType.REGULAR((2,)),
        ],
        compiler_params=pltpu.CompilerParams(collective_id=0, has_side_effects=True, vmem_limit_bytes=50331648),
    )(*(pltpu.with_memory_space_constraint(a, pltpu.HBM) for a in (fisher, factor_left, factor_right, base_weight)))


def solution(mesh):
    placed = (
        P("lang", None, "blk"),
        P("lang", "blk", None),
        P("lang", None, "blk"),
        P(("lang", "blk"), None),
    )
    return jax.shard_map(
        shards, mesh=mesh, in_specs=placed, out_specs=P(("lang", "blk"), None), check_vma=False
    )
```
